32 devices in a mesh: row: 4 (over y, x), col: 8 (over z, core).
Axes of the slice: x: 2, y: 2, z: 4, core: 2. Of those that a mesh axis runs over, the one named last changes fastest.
Arguments:
- object_tiles: float32 [2, 2, 1024, 2048], P(None, None, 'row', 'col'), may hold values from -5 to 5
- probe_modes: float32 [2, 4, 128, 128], replicated, may hold values from -6 to 6
- offsets: int32 [4, 8, 3, 2], P('row', 'col'), may hold values from 0 to 192
- amplitude: float32 [4, 8, 3, 128, 128], P('row', 'col'), may hold values from 0.2 to 3
Outputs:
- object_grad: float32 [2, 2, 1024, 2048], P(None, None, 'row', 'col')
- probe_new: float32 [2, 4, 128, 128], replicated
The draws below stay inside these ranges and needn't reach their ends.
All inputs are finite; a program needn't handle non-finite values.
Results may differ from the reference program's by a relative error of at most 0.0003.
Values sent between devices are 32-bit elements; how exact they have to be, the bound alone decides.
A program may use at most 64 MiB of HBM per device.

```python
import jax
import jax.numpy as jnp
from jax import lax

TILE = 256
HALO = 32
WIN = 128
MODES = 4
SLICES = 2
SCANS = 3
OBJ_ROWS = 1024
OBJ_COLS = 2048
N_ROW = 4
N_COL = 8


def plant(entries, key, least, top_value):
    shape = entries.shape
    index_at = [jax.random.randint(jax.random.fold_in(key, axis), (), 0, shape[axis]) for axis in range(len(shape))]
    entries = entries.at[tuple(index_at)].set(least)
    longest = shape.index(max(shape))
    index_at[longest] = (index_at[longest] + 1) % shape[longest]
    return entries.at[tuple(index_at)].set(top_value)


def block_scale(stream_key, dims, shards, low, top_value):
    def one(position, shards_of):
        heights = jax.random.uniform(jax.random.fold_in(jax.random.fold_in(stream_key, 6), position), (shards_of,), jnp.float32, low / len(shards), top_value / len(shards))
        return jnp.repeat(jnp.exp(heights), dims[position] // shards_of).reshape((-1,) + (1,) * (len(dims) - position - 1))

    gain = one(*shards[0])
    for cut in shards[1:]:
        gain = gain * one(*cut)
    return gain


def centred(own_key, extent, spread, limit, cuts=(), held_as=jnp.bfloat16):
    drawn = spread * jax.random.normal(own_key, extent, jnp.float32)
    if cuts:
        drawn = drawn * block_scale(own_key, extent, cuts, -0.22, 0.18)
    return jnp.clip(drawn, -limit, limit).astype(held_as)


def setup_inputs(seed: int = 0) -> dict:
    splits = jax.random.split(jax.random.key(seed), 5)
    return {
        "object_tiles": centred(splits[0], (2, SLICES, OBJ_ROWS, OBJ_COLS), 0.7, 5.0, ((2, 4), (3, 8)), jnp.float32),
        "probe_modes": centred(splits[1], (2, MODES, WIN, WIN), 1.0, 6.0, (), jnp.float32),
        "offsets": plant(jax.random.randint(splits[2], (N_ROW, N_COL, SCANS, 2), 0, TILE + 2 * HALO - WIN + 1), jax.random.fold_in(splits[2], 1), 0, TILE + 2 * HALO - WIN).astype(jnp.int32),
        "amplitude": jnp.clip(0.2 + 2.8 * jax.random.uniform(splits[3], (N_ROW, N_COL, SCANS, WIN, WIN), jnp.float32) ** block_scale(splits[3], (N_ROW, N_COL, SCANS, WIN, WIN), ((0, 4), (1, 8)), -0.2, 0.2), 0.2, 3.0),
    }


PROP = 0.002
SHIFT_AMP = 0.5
STEP_SIZE = 0.5
EPSILON = 1e-06
HIGH = lax.Precision.HIGHEST

def tables():
    counter = jnp.arange(WIN, dtype=jnp.int32)
    product = counter[:, None] * counter[None, :] % WIN
    angles = product.astype(jnp.float32) * (2.0 * jnp.pi / WIN)
    scale_factor = 1.0 / jnp.sqrt(jnp.float32(WIN))
    cos_table = jnp.cos(angles) * scale_factor
    sin_table = jnp.sin(angles) * scale_factor
    frequency = ((counter + WIN // 2) % WIN - WIN // 2).astype(jnp.float32)
    phase_map = -PROP * (frequency[:, None] ** 2 + frequency[None, :] ** 2)
    return (cos_table, sin_table, jnp.cos(phase_map), jnp.sin(phase_map))

def matprod(left_op, right_op):
    return jnp.matmul(left_op, right_op, precision=HIGH)

def transform(wave_real, wave_imag, sign_value, cos_table, sin_table):
    first_real = matprod(cos_table, wave_real) + sign_value * matprod(sin_table, wave_imag)
    first_imag = matprod(cos_table, wave_imag) - sign_value * matprod(sin_table, wave_real)
    second_real = matprod(first_real, cos_table) + sign_value * matprod(first_imag, sin_table)
    second_imag = matprod(first_imag, cos_table) - sign_value * matprod(first_real, sin_table)
    return (second_real, second_imag)

def position_loss(window, probe_field, measured, table_set):
    cos_table, sin_table, prop_cos, prop_sin = table_set
    probe_real = probe_field[0]
    probe_imag = probe_field[1]
    wave_real = probe_real * window[0, 0] - probe_imag * window[1, 0]
    wave_imag = probe_real * window[1, 0] + probe_imag * window[0, 0]
    for layer_no in range(1, SLICES):
        wave_real, wave_imag = transform(wave_real, wave_imag, 1.0, cos_table, sin_table)
        turned_real = wave_real * prop_cos - wave_imag * prop_sin
        turned_imag = wave_real * prop_sin + wave_imag * prop_cos
        wave_real, wave_imag = transform(turned_real, turned_imag, -1.0, cos_table, sin_table)
        slice_real = window[0, layer_no]
        slice_imag = window[1, layer_no]
        wave_real, wave_imag = (wave_real * slice_real - wave_imag * slice_imag, wave_real * slice_imag + wave_imag * slice_real)
    far_real, far_imag = transform(wave_real, wave_imag, 1.0, cos_table, sin_table)
    intensity = lax.optimization_barrier(jnp.sum(far_real * far_real + far_imag * far_imag, axis=0))
    return jnp.sum((jnp.sqrt(intensity + SHIFT_AMP) - measured) ** 2)

def update_probe(probe_field, gradient):
    mean_square = jnp.sum(gradient * gradient) / (2 * MODES * WIN * WIN)
    return probe_field - STEP_SIZE * gradient / jnp.sqrt(mean_square + EPSILON)

def reference(object_tiles, probe_modes, offsets, amplitude):
    table_set = tables()
    obj_rows = object_tiles.shape[2]
    obj_cols = object_tiles.shape[3]
    flat_offsets = offsets.reshape(-1, 2)
    flat_amp = amplitude.reshape(-1, WIN, WIN)
    numbers = jnp.arange(flat_offsets.shape[0], dtype=jnp.int32)
    window_span = jnp.arange(WIN, dtype=jnp.int32)

    def total_loss(tiles_field, probe_field):

        def step_fn(loss_acc, scan_item):
            number, shift_pair, measured = scan_item
            grid_row = number // (N_COL * SCANS)
            grid_col = number // SCANS % N_COL
            row_start = grid_row * TILE - HALO + shift_pair[0]
            col_start = grid_col * TILE - HALO + shift_pair[1]
            row_index = ((row_start + window_span) % obj_rows).astype(jnp.int32)
            col_index = ((col_start + window_span) % obj_cols).astype(jnp.int32)
            window = jnp.take(jnp.take(tiles_field, row_index, axis=2), col_index, axis=3)
            return (loss_acc + position_loss(window, probe_field, measured, table_set), None)
        loss_sum, _ = lax.scan(step_fn, jnp.zeros((), jnp.float32), (numbers, flat_offsets, flat_amp))
        return loss_sum
    grad_tiles, grad_probe = jax.grad(total_loss, argnums=(0, 1))(object_tiles, probe_modes)
    return (grad_tiles, update_probe(probe_modes, grad_probe))
```

```python
import functools

import jax
import jax.numpy as jnp
import numpy as np
from jax import lax
from jax.experimental import pallas as pl
from jax.experimental.pallas import tpu as pltpu
from jax.sharding import PartitionSpec as P

HALO = 32
PROP = 0.002
SHIFT_AMP = 0.5
STEP_SIZE = 0.5
EPSILON = 1e-06
LANES = 128
SUB = 8
MESH = pl.DeviceIdType.MESH
F32 = jnp.float32
BF16 = jnp.bfloat16


def tables(win):
    k = np.arange(win)
    c = np.exp(-2j * np.pi * (k[:, None] * k[None, :] % win) / win) / np.sqrt(win)
    freq = (k + win // 2) % win - win // 2
    kern = np.conj(c) @ np.diag(np.exp(-1j * PROP * freq**2)) @ c
    out = []
    for m in (c, np.conj(c), kern, np.conj(kern)):
        full = np.block([[m.real, m.imag], [-m.imag, m.real]])
        high = full.astype(np.float32).astype(jnp.bfloat16)
        low = (full - high.astype(np.float64)).astype(np.float32).astype(jnp.bfloat16)
        out += [high, low]
    return np.stack(out)


FWD, INV, KER, KER_INV = 0, 1, 2, 3


def split(x):
    high = x.astype(BF16)
    return high, (x - high.astype(F32)).astype(BF16)


def dot(a, b):
    return jnp.dot(a, b, preferred_element_type=F32)


def right(x, tab, which):
    high, low = split(x)
    return dot(high, tab[2 * which]) + (
        dot(low, tab[2 * which]) + dot(high, tab[2 * which + 1])
    )


def left(x, tab, which):
    high, low = split(x)
    which = which ^ 1
    return dot(tab[2 * which], high) + (
        dot(tab[2 * which], low) + dot(tab[2 * which + 1], high)
    )


def swap(y):
    w = y.shape[0] // 2
    top = jnp.concatenate([y[:w, :w], y[w:, :w]], axis=1)
    low = jnp.concatenate([y[:w, w:], y[w:, w:]], axis=1)
    return jnp.concatenate([top, low], axis=0)


def twice(x, axis):
    return jnp.concatenate([x, x], axis=axis)


def lane(rows):
    return lax.broadcasted_iota(jnp.int32, (rows, LANES), 1)


CHANS = [(part, lay) for part in range(2) for lay in range(2)]
EVERY = slice(None)


def packed(get, first, rows):
    out = None
    for ch in range(4):
        shift = (HALO * ch - first) % LANES
        block = get(ch)
        block = pltpu.roll(block, shift, 1) if shift else block
        at = lane(rows)
        keep = (at >= HALO * ch) & (at < HALO * ch + HALO)
        out = jnp.where(keep, block, 0.0 if out is None else out)
    return out


def unpacked(block, ch, first):
    shift = (first - HALO * ch) % LANES
    return pltpu.roll(block, shift, 1) if shift else block


def send(src, dst, ssem, rsem, i, to):
    copy = pltpu.make_async_remote_copy(
        src_ref=src,
        dst_ref=dst,
        send_sem=ssem.at[i],
        recv_sem=rsem.at[i],
        device_id=to,
        device_id_type=MESH,
    )
    copy.start()
    return copy


def places(n_row, n_col):
    my_r = lax.axis_index("row")
    my_c = lax.axis_index("col")
    up = lax.rem(my_r + n_row - 1, n_row)
    down = lax.rem(my_r + 1, n_row)
    lft = lax.rem(my_c + n_col - 1, n_col)
    rgt = lax.rem(my_c + 1, n_col)
    return my_r, my_c, up, down, lft, rgt


def zones(tile):
    head, tail = pl.ds(0, HALO), pl.ds(tile - HALO, HALO)
    mid, after, body = pl.ds(HALO, tile), pl.ds(HALO + tile, HALO), pl.ds(0, tile)
    return head, tail, mid, after, body


def rows_of(p, win):
    return [[(4 * p + 2 * part + m) * win for m in range(2)] for part in range(2)]


def halo_kernel(
    sizes, obj_ref, ext, pack_l, pack_r, halo_l, halo_r, h_send, h_recv
):
    n_row, n_col = sizes
    tile = obj_ref.shape[2]
    tall = tile + 2 * HALO
    wide = tile + LANES
    my_r, my_c, up, down, lft, rgt = places(n_row, n_col)
    head, tail, mid, after, body = zones(tile)
    barrier = pltpu.get_barrier_semaphore()
    around = [(r, c) for r in (up, my_r, down) for c in (lft, my_c, rgt)]
    del around[4]
    for to in around:
        pl.semaphore_signal(barrier, inc=1, device_id=to, device_id_type=MESH)
    pack_l[...] = packed(lambda ch: obj_ref[CHANS[ch] + (EVERY, slice(0, LANES))], 0, tile)
    pack_r[...] = packed(
        lambda ch: obj_ref[CHANS[ch] + (EVERY, slice(tile - LANES, tile))], LANES - HALO, tile
    )
    pl.semaphore_wait(barrier, 8)
    halo = [
        send(obj_ref.at[:, :, tail, :], ext.at[:, :, head, body], h_send, h_recv, 0, (down, my_c)),
        send(obj_ref.at[:, :, head, :], ext.at[:, :, after, body], h_send, h_recv, 1, (up, my_c)),
        send(pack_r, halo_l.at[mid], h_send, h_recv, 2, (my_r, rgt)),
        send(pack_l, halo_r.at[mid], h_send, h_recv, 3, (my_r, lft)),
        send(pack_r.at[tail], halo_l.at[head], h_send, h_recv, 4, (down, rgt)),
        send(pack_r.at[head], halo_l.at[after], h_send, h_recv, 5, (up, rgt)),
        send(pack_l.at[tail], halo_r.at[head], h_send, h_recv, 6, (down, lft)),
        send(pack_l.at[head], halo_r.at[after], h_send, h_recv, 7, (up, lft)),
    ]
    ext[:, :, mid, body] = obj_ref[...]
    ext[:, :, pl.ds(tall, SUB), :] = jnp.zeros((2, 2, SUB, wide), F32)
    for copy in halo:
        copy.wait()
    for ch in range(4):
        near = unpacked(halo_r[...], ch, 0)
        far_side = unpacked(halo_l[...], ch, LANES - HALO)
        at = lane(tall)
        edge = jnp.where(at < HALO, near, jnp.where(at >= LANES - HALO, far_side, 0.0))
        ext[CHANS[ch] + (pl.ds(0, tall), pl.ds(tile, LANES))] = edge


def local_kernel(
    sizes, off_ref, ext, probe_ref, amp_ref, tab, acc, gprobe, winds, wave, far, factor, gobj
):
    win, scans = sizes
    wide = ext.shape[3]
    acc[...] = jnp.zeros_like(acc)
    gprobe[...] = jnp.zeros_like(gprobe)
    gobj[...] = jnp.zeros_like(gobj)

    @pl.loop(0, scans)
    def _(s):
        row = off_ref[0, 0, s, 0]
        base = pl.multiple_of(row - lax.rem(row, SUB), SUB)
        rest = lax.rem(win + SUB - lax.rem(row, SUB), win + SUB)
        shift = lax.rem(wide + HALO - off_ref[0, 0, s, 1], wide)
        o = {}
        for ch, (part, lay) in enumerate(CHANS):
            block = ext[part, lay, pl.ds(base, win + SUB), :]
            block = pltpu.roll(block, shift, 1)[:, :win]
            o[part, lay] = pltpu.roll(block, rest, 0)[:win]
            winds[s, ch] = o[part, lay]
        power = None
        for p in range(2):
            rows = []
            for m in range(2):
                pr, pi = probe_ref[0, 2 * p + m], probe_ref[1, 2 * p + m]
                rows.append(
                    jnp.concatenate(
                        [
                            pr * o[0, 0] - pi * o[1, 0],
                            pr * o[1, 0] + pi * o[0, 0],
                        ],
                        axis=1,
                    )
                )
            psi = jnp.concatenate(rows, axis=0)
            w = left(swap(right(psi, tab, KER)), tab, KER)
            wave[s, p] = w
            wr, wi = w[:win], w[win:]
            o1r, o1i = twice(o[0, 1], 1), twice(o[1, 1], 1)
            psi = jnp.concatenate([wr * o1r - wi * o1i, wr * o1i + wi * o1r], axis=0)
            psi = right(swap(left(psi, tab, FWD)), tab, FWD)
            far[s, p] = psi
            sq = psi * psi
            part_sum = (sq[:win, :win] + sq[:win, win:]) + (sq[win:, :win] + sq[win:, win:])
            power = part_sum if power is None else power + part_sum
        root = jnp.sqrt(power + SHIFT_AMP)
        factor[s] = 2.0 * (root - amp_ref[0, 0, s]) / root

    def backward(p, s):
        f = factor[s]
        g = far[s, p] * twice(twice(f, 0), 1)
        g = left(swap(right(g, tab, INV)), tab, INV)
        w = wave[s, p]
        gr, gi, wr, wi = g[:win], g[win:], w[:win], w[win:]
        re = wr * gr + wi * gi
        im = wr * gi - wi * gr
        gobj[s, 1] += re[:, :win] + re[:, win:]
        gobj[s, 3] += im[:, :win] + im[:, win:]
        o1r, o1i = twice(winds[s, 1], 1), twice(winds[s, 3], 1)
        g = jnp.concatenate([o1r * gr + o1i * gi, o1r * gi - o1i * gr], axis=0)
        g = right(swap(left(g, tab, KER_INV)), tab, KER_INV)
        o0r, o0i = winds[s, 0], winds[s, 2]
        re = im = None
        for m in range(2):
            gr, gi = g[m * win : (m + 1) * win, :win], g[m * win : (m + 1) * win, win:]
            pr, pi = probe_ref[0, 2 * p + m], probe_ref[1, 2 * p + m]
            a = pr * gr + pi * gi
            b = pr * gi - pi * gr
            re, im = (a, b) if re is None else (re + a, im + b)
            at = rows_of(p, win)
            gprobe[pl.ds(at[0][m], win)] += o0r * gr + o0i * gi
            gprobe[pl.ds(at[1][m], win)] += o0r * gi - o0i * gr
        gobj[s, 0] += re
        gobj[s, 2] += im

    @pl.loop(0, scans)
    def _(s):
        backward(0, s)

    @pl.loop(0, scans)
    def _(s):
        backward(1, s)
        row = off_ref[0, 0, s, 0]
        rest = lax.rem(row, SUB)
        base = pl.multiple_of(row - rest, SUB)
        shift = lax.rem(wide - HALO + off_ref[0, 0, s, 1], wide)
        for ch, (part, lay) in enumerate(CHANS):
            block = jnp.concatenate([gobj[s, ch], jnp.zeros((SUB, win), F32)], axis=0)
            block = pltpu.roll(block, rest, 0)
            block = jnp.concatenate([block, jnp.zeros((win + SUB, wide - win), F32)], axis=1)
            acc[part, lay, pl.ds(base, win + SUB), :] += pltpu.roll(block, shift, 1)


def sum_kernel(
    sizes,
    acc,
    gprobe,
    probe_ref,
    grad_ref,
    new_ref,
    total,
    from_top,
    from_bot,
    edge_l,
    edge_r,
    from_l,
    from_r,
    parts,
    g_send,
    g_recv,
    rs_send,
    rs_recv,
    ag_send,
    ag_recv,
):
    n_row, n_col, chunks = sizes
    n_dev = n_row * n_col
    tile, win = grad_ref.shape[2], probe_ref.shape[2]
    tall = tile + 2 * HALO
    my_r, my_c, up, down, lft, rgt = places(n_row, n_col)
    head, tail, mid, after, body = zones(tile)
    me = my_r * n_col + my_c

    def peer(k):
        other = lax.rem(me + k, n_dev)
        return other, (other // n_col, lax.rem(other, n_col))

    barrier = pltpu.get_barrier_semaphore()

    @pl.loop(1, n_dev)
    def _(k):
        pl.semaphore_signal(barrier, inc=1, device_id=peer(k)[1], device_id_type=MESH)

    tall_rows = pl.ds(0, tall)
    edge_of = lambda ch: acc[CHANS[ch] + (tall_rows, pl.ds(tile, LANES))]
    edge_r[...] = packed(edge_of, 0, tall)
    edge_l[...] = packed(edge_of, LANES - HALO, tall)
    pl.semaphore_wait(barrier, n_dev - 1)

    n_rows = gprobe.shape[0] // chunks
    piece = n_rows // n_dev

    def scatter_start(c):
        @pl.loop(1, n_dev)
        def _(k):
            other, where = peer(k)
            send(
                gprobe.at[pl.ds(pl.multiple_of(c * n_rows + other * piece, piece), piece)],
                parts.at[c, pl.ds(pl.multiple_of((k - 1) * piece, piece), piece)],
                rs_send,
                rs_recv,
                c,
                where,
            )

    mine = [
        pl.ds(pl.multiple_of(c * n_rows + me * piece, piece), piece) for c in range(chunks)
    ]

    def wait_all(sem, ref):
        pltpu.make_async_copy(ref, ref, sem).wait()

    def gather_start(c):
        wait_all(rs_recv.at[c], parts.at[c])
        value = gprobe[mine[c]]
        for k in range(n_dev - 1):
            value = value + parts[c, pl.ds(k * piece, piece)]
        total[mine[c]] = value

        @pl.loop(1, n_dev)
        def _(k):
            _, where = peer(k)
            send(total.at[mine[c]], total.at[mine[c]], ag_send, ag_recv, c, where)

    for c in range(chunks):
        scatter_start(c)
    grads = [
        send(acc.at[:, :, head, body], from_bot, g_send, g_recv, 0, (up, my_c)),
        send(acc.at[:, :, after, body], from_top, g_send, g_recv, 1, (down, my_c)),
        send(edge_r.at[mid], from_l.at[mid], g_send, g_recv, 2, (my_r, rgt)),
        send(edge_l.at[mid], from_r.at[mid], g_send, g_recv, 3, (my_r, lft)),
        send(edge_r.at[head], from_l.at[after], g_send, g_recv, 4, (up, rgt)),
        send(edge_r.at[after], from_l.at[head], g_send, g_recv, 5, (down, rgt)),
        send(edge_l.at[head], from_r.at[after], g_send, g_recv, 6, (up, lft)),
        send(edge_l.at[after], from_r.at[head], g_send, g_recv, 7, (down, lft)),
    ]
    for c in range(chunks):
        gather_start(c)
    grad_ref[...] = acc[:, :, mid, body]
    for copy in grads:
        copy.wait()
    grad_ref[:, :, head, :] += from_top[...]
    grad_ref[:, :, tail, :] += from_bot[...]
    for ref, first, cols in (
        (from_l, 0, pl.ds(0, LANES)),
        (from_r, LANES - HALO, pl.ds(tile - LANES, LANES)),
    ):
        for ch in range(4):
            at = lane(tall)
            block = unpacked(ref[...], ch, first)
            block = jnp.where((at >= first) & (at < first + HALO), block, 0.0)
            part, lay = CHANS[ch]
            grad_ref[part, lay, :, cols] += block[HALO : HALO + tile]
            grad_ref[part, lay, head, cols] += block[:HALO]
            grad_ref[part, lay, tail, cols] += block[HALO + tile :]
    for c in range(chunks):
        wait_all(ag_recv.at[c], parts.at[c])
    full = total[...]
    scale = STEP_SIZE / jnp.sqrt(jnp.sum(full * full, keepdims=True) / full.size + EPSILON)
    for p in range(2):
        for part in range(2):
            for m in range(2):
                at = rows_of(p, win)[part][m]
                new_ref[part, 2 * p + m] = (
                    probe_ref[part, 2 * p + m] - scale * total[pl.ds(at, win)]
                )
    for c in range(chunks):
        wait_all(rs_send.at[c], parts.at[c])
        wait_all(ag_send.at[c], parts.at[c])


def on_device(object_tiles, probe_modes, offsets, amplitude):
    n_row, n_col = lax.axis_size("row"), lax.axis_size("col")
    n_dev = n_row * n_col
    tile, win, scans = object_tiles.shape[2], probe_modes.shape[2], offsets.shape[2]
    tall, wide = tile + 2 * HALO, tile + LANES
    g_rows = 2 * probe_modes.shape[1] * win
    chunks = 2 if g_rows // 2 % (8 * n_dev) == 0 else 1
    piece = g_rows // chunks // n_dev
    vmem = pl.BlockSpec(memory_space=pltpu.VMEM)
    smem = pl.BlockSpec(memory_space=pltpu.SMEM)
    dma = pltpu.SemaphoreType.DMA
    side = pltpu.VMEM((tall, LANES), F32)
    wide_tile = jax.ShapeDtypeStruct((2, 2, tall + SUB, wide), F32)
    limit = 40 * 1024 * 1024
    ext = pl.pallas_call(
        functools.partial(halo_kernel, (n_row, n_col)),
        out_shape=wide_tile,
        in_specs=[vmem],
        out_specs=vmem,
        scratch_shapes=[
            pltpu.VMEM((tile, LANES), F32),
            pltpu.VMEM((tile, LANES), F32),
            side,
            side,
            dma((8,)),
            dma((8,)),
        ],
        compiler_params=pltpu.CompilerParams(
            collective_id=0, has_side_effects=True, vmem_limit_bytes=limit
        ),
    )(object_tiles)
    acc, gprobe = pl.pallas_call(
        functools.partial(local_kernel, (win, scans)),
        out_shape=(wide_tile, jax.ShapeDtypeStruct((g_rows, win), F32)),
        in_specs=[smem] + [vmem] * 4,
        out_specs=(vmem, vmem),
        scratch_shapes=[
            pltpu.VMEM((scans, 4, win, win), F32),
            pltpu.VMEM((scans, 2, 2 * win, 2 * win), F32),
            pltpu.VMEM((scans, 2, 2 * win, 2 * win), F32),
            pltpu.VMEM((scans, win, win), F32),
            pltpu.VMEM((scans, 4, win, win), F32),
        ],
        compiler_params=pltpu.CompilerParams(vmem_limit_bytes=limit),
    )(offsets, ext, probe_modes, amplitude, jnp.asarray(tables(win)))
    return pl.pallas_call(
        functools.partial(sum_kernel, (n_row, n_col, chunks)),
        out_shape=(
            jax.ShapeDtypeStruct(object_tiles.shape, F32),
            jax.ShapeDtypeStruct(probe_modes.shape, F32),
        ),
        in_specs=[vmem] * 3,
        out_specs=(vmem, vmem),
        scratch_shapes=[
            pltpu.VMEM((g_rows, win), F32),
            pltpu.VMEM((2, 2, HALO, tile), F32),
            pltpu.VMEM((2, 2, HALO, tile), F32),
            side,
            side,
            side,
            side,
            pltpu.VMEM((chunks, (n_dev - 1) * piece, win), F32),
            dma((8,)),
            dma((8,)),
            dma((chunks,)),
            dma((chunks,)),
            dma((chunks,)),
            dma((chunks,)),
        ],
        compiler_params=pltpu.CompilerParams(
            collective_id=1, has_side_effects=True, vmem_limit_bytes=limit
        ),
    )(acc, gprobe, probe_modes)


def solution(mesh):
    placed = (
        P(None, None, "row", "col"),
        P(),
        P("row", "col", None, None),
        P("row", "col", None, None, None),
    )
    return jax.shard_map(
        on_device,
        mesh=mesh,
        in_specs=placed,
        out_specs=(P(None, None, "row", "col"), P()),
        check_vma=False,
    )
```

```python
import functools

import jax
import jax.numpy as jnp
import numpy as np
from jax import lax
from jax.experimental import pallas as pl
from jax.experimental.pallas import tpu as pltpu
from jax.sharding import PartitionSpec as P

HALO = 32
PROP = 0.002
SHIFT_AMP = 0.5
STEP_SIZE = 0.5
EPSILON = 1e-06
LANES = 128
SUB = 8
MESH = pl.DeviceIdType.MESH
F32 = jnp.float32
BF16 = jnp.bfloat16


def tables(win):
    k = np.arange(win)
    c = np.exp(-2j * np.pi * (k[:, None] * k[None, :] % win) / win) / np.sqrt(win)
    freq = (k + win // 2) % win - win // 2
    kern = np.conj(c) @ np.diag(np.exp(-1j * PROP * freq**2)) @ c
    out = []
    for m in (c, np.conj(c), kern, np.conj(kern)):
        full = np.block([[m.real, m.imag], [-m.imag, m.real]])
        high = full.astype(np.float32).astype(jnp.bfloat16)
        low = (full - high.astype(np.float64)).astype(np.float32).astype(jnp.bfloat16)
        out += [high, low]
    return np.stack(out)


FWD, INV, KER, KER_INV = 0, 1, 2, 3


def split(x):
    high = x.astype(BF16)
    return high, (x - high.astype(F32)).astype(BF16)


def dot(a, b):
    return jnp.dot(a, b, preferred_element_type=F32)


def right(x, tab, which):
    high, low = split(x)
    return dot(high, tab[2 * which]) + (
        dot(low, tab[2 * which]) + dot(high, tab[2 * which + 1])
    )


def left(x, tab, which):
    high, low = split(x)
    which = which ^ 1
    return dot(tab[2 * which], high) + (
        dot(tab[2 * which], low) + dot(tab[2 * which + 1], high)
    )


def swap(y):
    w = y.shape[0] // 2
    top = jnp.concatenate([y[:w, :w], y[w:, :w]], axis=1)
    low = jnp.concatenate([y[:w, w:], y[w:, w:]], axis=1)
    return jnp.concatenate([top, low], axis=0)


def twice(x, axis):
    return jnp.concatenate([x, x], axis=axis)


def lane(rows):
    return lax.broadcasted_iota(jnp.int32, (rows, LANES), 1)


CHANS = [(part, lay) for part in range(2) for lay in range(2)]
EVERY = slice(None)


def packed(get, first, rows, count=4):
    out = None
    for ch in range(count):
        shift = (HALO * ch - first) % LANES
        block = get(ch)
        block = pltpu.roll(block, shift, 1) if shift else block
        at = lane(rows)
        keep = (at >= HALO * ch) & (at < HALO * ch + HALO)
        out = jnp.where(keep, block, 0.0 if out is None else out)
    return out


def unpacked(block, ch, first):
    shift = (first - HALO * ch) % LANES
    return pltpu.roll(block, shift, 1) if shift else block


def send(src, dst, ssem, rsem, i, to):
    copy = pltpu.make_async_remote_copy(
        src_ref=src,
        dst_ref=dst,
        send_sem=ssem.at[i],
        recv_sem=rsem.at[i],
        device_id=to,
        device_id_type=MESH,
    )
    copy.start()
    return copy


def places(n_row, n_col):
    my_r = lax.axis_index("row")
    my_c = lax.axis_index("col")
    up = lax.rem(my_r + n_row - 1, n_row)
    down = lax.rem(my_r + 1, n_row)
    lft = lax.rem(my_c + n_col - 1, n_col)
    rgt = lax.rem(my_c + 1, n_col)
    return my_r, my_c, up, down, lft, rgt


def zones(tile):
    head, tail = pl.ds(0, HALO), pl.ds(tile - HALO, HALO)
    mid, after, body = pl.ds(HALO, tile), pl.ds(HALO + tile, HALO), pl.ds(0, tile)
    return head, tail, mid, after, body


def rows_of(p, win):
    return [[(4 * p + 2 * part + m) * win for m in range(2)] for part in range(2)]


def halo_kernel(
    sizes, obj_ref, ext, pack_l, pack_r, halo_l, halo_r, h_send, h_recv
):
    n_row, n_col = sizes
    tile = obj_ref.shape[2]
    tall = tile + 2 * HALO
    wide = tile + LANES
    my_r, my_c, up, down, lft, rgt = places(n_row, n_col)
    head, tail, mid, after, body = zones(tile)
    barrier = pltpu.get_barrier_semaphore()
    around = [(r, c) for r in (up, my_r, down) for c in (lft, my_c, rgt)]
    del around[4]
    for to in around:
        pl.semaphore_signal(barrier, inc=1, device_id=to, device_id_type=MESH)
    pack_l[...] = packed(lambda ch: obj_ref[CHANS[ch] + (EVERY, slice(0, LANES))], 0, tile)
    pack_r[...] = packed(
        lambda ch: obj_ref[CHANS[ch] + (EVERY, slice(tile - LANES, tile))], LANES - HALO, tile
    )
    pl.semaphore_wait(barrier, 8)
    halo = [
        send(obj_ref.at[:, :, tail, :], ext.at[:, :, head, body], h_send, h_recv, 0, (down, my_c)),
        send(obj_ref.at[:, :, head, :], ext.at[:, :, after, body], h_send, h_recv, 1, (up, my_c)),
        send(pack_r, halo_l.at[mid], h_send, h_recv, 2, (my_r, rgt)),
        send(pack_l, halo_r.at[mid], h_send, h_recv, 3, (my_r, lft)),
        send(pack_r.at[tail], halo_l.at[head], h_send, h_recv, 4, (down, rgt)),
        send(pack_r.at[head], halo_l.at[after], h_send, h_recv, 5, (up, rgt)),
        send(pack_l.at[tail], halo_r.at[head], h_send, h_recv, 6, (down, lft)),
        send(pack_l.at[head], halo_r.at[after], h_send, h_recv, 7, (up, lft)),
    ]
    ext[:, :, mid, body] = obj_ref[...]
    ext[:, :, pl.ds(tall, SUB), :] = jnp.zeros((2, 2, SUB, wide), F32)
    for copy in halo:
        copy.wait()
    for ch in range(4):
        near = unpacked(halo_r[...], ch, 0)
        far_side = unpacked(halo_l[...], ch, LANES - HALO)
        at = lane(tall)
        edge = jnp.where(at < HALO, near, jnp.where(at >= LANES - HALO, far_side, 0.0))
        ext[CHANS[ch] + (pl.ds(0, tall), pl.ds(tile, LANES))] = edge


def window_kernel(sizes, off_ref, ext, winds):
    win, scans = sizes
    wide = ext.shape[3]

    @pl.loop(0, scans)
    def _(s):
        row = off_ref[0, 0, s, 0]
        base = pl.multiple_of(row - lax.rem(row, SUB), SUB)
        rest = lax.rem(win + SUB - lax.rem(row, SUB), win + SUB)
        shift = lax.rem(wide + HALO - off_ref[0, 0, s, 1], wide)
        for ch, (part, lay) in enumerate(CHANS):
            block = ext[part, lay, pl.ds(base, win + SUB), :]
            block = pltpu.roll(block, shift, 1)[:, :win]
            winds[s, ch] = pltpu.roll(block, rest, 0)[:win]


def main_kernel(
    sizes,
    off_ref,
    winds,
    probe_ref,
    amp_ref,
    tab,
    grad_ref,
    new_ref,
    wave,
    far,
    factor,
    gobj,
    gprobe,
    acc,
    total,
    spread,
    from_top,
    from_bot,
    edge_l,
    edge_r,
    from_l,
    from_r,
    half_in,
    half_sum,
    parts,
    g_send,
    g_recv,
    pair_send,
    pair_recv,
    rs_send,
    rs_recv,
    ag_send,
    ag_recv,
    fw_send,
    fw_recv,
):
    n_row, n_col, win, scans, chunks = sizes
    n_dev = n_row * n_col
    n_half = n_col // 2
    group = n_row * n_half
    tile = grad_ref.shape[2]
    tall, wide = tile + 2 * HALO, tile + LANES
    my_r, my_c, up, down, lft, rgt = places(n_row, n_col)
    head, tail, mid, after, body = zones(tile)
    me = my_r * n_col + my_c
    barrier = pltpu.get_barrier_semaphore()

    @pl.loop(1, n_dev)
    def _(k):
        other = lax.rem(me + k, n_dev)
        where = (other // n_col, lax.rem(other, n_col))
        pl.semaphore_signal(barrier, inc=1, device_id=where, device_id_type=MESH)

    gprobe[...] = jnp.zeros_like(gprobe)
    gobj[...] = jnp.zeros_like(gobj)

    @pl.loop(0, scans)
    def _(s):
        o = {chan: winds[s, ch] for ch, chan in enumerate(CHANS)}
        power = None
        for p in range(2):
            rows = []
            for m in range(2):
                pr, pi = probe_ref[0, 2 * p + m], probe_ref[1, 2 * p + m]
                rows.append(
                    jnp.concatenate(
                        [
                            pr * o[0, 0] - pi * o[1, 0],
                            pr * o[1, 0] + pi * o[0, 0],
                        ],
                        axis=1,
                    )
                )
            psi = jnp.concatenate(rows, axis=0)
            w = left(swap(right(psi, tab, KER)), tab, KER)
            wave[s, p] = w
            wr, wi = w[:win], w[win:]
            o1r, o1i = twice(o[0, 1], 1), twice(o[1, 1], 1)
            psi = jnp.concatenate([wr * o1r - wi * o1i, wr * o1i + wi * o1r], axis=0)
            psi = right(swap(left(psi, tab, FWD)), tab, FWD)
            far[s, p] = psi
            sq = psi * psi
            part_sum = (sq[:win, :win] + sq[:win, win:]) + (sq[win:, :win] + sq[win:, win:])
            power = part_sum if power is None else power + part_sum
        root = jnp.sqrt(power + SHIFT_AMP)
        factor[s] = 2.0 * (root - amp_ref[0, 0, s]) / root


    def first_half(p, s):
        g = far[s, p] * twice(twice(factor[s], 0), 1)
        g = left(swap(right(g, tab, INV)), tab, INV)
        w = wave[s, p]
        gr, gi, wr, wi = g[:win], g[win:], w[:win], w[win:]
        re = wr * gr + wi * gi
        im = wr * gi - wi * gr
        gobj[1, 0, s] += re[:, :win] + re[:, win:]
        gobj[1, 1, s] += im[:, :win] + im[:, win:]
        o1r, o1i = twice(winds[s, 1], 1), twice(winds[s, 3], 1)
        far[s, p] = jnp.concatenate([o1r * gr + o1i * gi, o1r * gi - o1i * gr], axis=0)

    def second_half(p, s):
        g = right(swap(left(far[s, p], tab, KER_INV)), tab, KER_INV)
        o0r, o0i = winds[s, 0], winds[s, 2]
        re = im = None
        for m in range(2):
            gr, gi = g[m * win : (m + 1) * win, :win], g[m * win : (m + 1) * win, win:]
            pr, pi = probe_ref[0, 2 * p + m], probe_ref[1, 2 * p + m]
            a = pr * gr + pi * gi
            b = pr * gi - pi * gr
            re, im = (a, b) if re is None else (re + a, im + b)
            at = rows_of(p, win)
            gprobe[pl.ds(at[0][m], win)] += o0r * gr + o0i * gi
            gprobe[pl.ds(at[1][m], win)] += o0r * gi - o0i * gr
        gobj[0, 0, s] += re
        gobj[0, 1, s] += im

    def one_hot(at, target):
        return jnp.where(at == target, 1.0, 0.0).astype(BF16)

    def place(lay):
        for s in range(scans):
            k = lax.broadcasted_iota(jnp.int32, (win, wide), 0) + (off_ref[0, 0, s, 1] - HALO)
            k = jnp.where(k < 0, k + wide, k)
            cols = one_hot(lax.broadcasted_iota(jnp.int32, (win, wide), 1), k)
            for part in range(2):
                for t, term in enumerate(split(gobj[lay, part, s])):
                    spread[t, pl.ds(s * win, win), pl.ds(part * wide, wide)] = dot(
                        term, cols
                    ).astype(BF16)
        rows = []
        for s in range(scans):
            j = lax.broadcasted_iota(jnp.int32, (tall, win), 1) + off_ref[0, 0, s, 0]
            rows.append(one_hot(lax.broadcasted_iota(jnp.int32, (tall, win), 0), j))
        rows = jnp.concatenate(rows, axis=1)
        for part in range(2):
            cut = pl.ds(part * wide, wide)
            acc[part, lay] = dot(rows, spread[0, :, cut]) + dot(rows, spread[1, :, cut])

    def grads_start(lay):
        edge_of = lambda ch: acc[ch, lay, :, pl.ds(tile, LANES)]
        er, el, fl, fr = edge_r.at[lay], edge_l.at[lay], from_l.at[lay], from_r.at[lay]
        er[...] = packed(edge_of, 0, tall, 2)
        el[...] = packed(edge_of, LANES - HALO, tall, 2)
        ss, rs = g_send.at[lay], g_recv.at[lay]
        return [
            send(acc.at[:, lay, head, body], from_bot.at[lay], ss, rs, 0, (up, my_c)),
            send(acc.at[:, lay, after, body], from_top.at[lay], ss, rs, 1, (down, my_c)),
            send(er.at[mid], fl.at[mid], ss, rs, 2, (my_r, rgt)),
            send(el.at[mid], fr.at[mid], ss, rs, 3, (my_r, lft)),
            send(er.at[head], fl.at[after], ss, rs, 4, (up, rgt)),
            send(er.at[after], fl.at[head], ss, rs, 5, (down, rgt)),
            send(el.at[head], fr.at[after], ss, rs, 6, (up, lft)),
            send(el.at[after], fr.at[head], ss, rs, 7, (down, lft)),
        ]

    def grads_end(lay, copies):
        grad_ref[:, lay] = acc[:, lay, mid, body]
        for copy in copies:
            copy.wait()
        grad_ref[:, lay, head, :] += from_top[lay]
        grad_ref[:, lay, tail, :] += from_bot[lay]
        for ref, first, cols in (
            (from_l, 0, pl.ds(0, LANES)),
            (from_r, LANES - HALO, pl.ds(tile - LANES, LANES)),
        ):
            for ch in range(2):
                at = lane(tall)
                block = unpacked(ref[lay], ch, first)
                block = jnp.where((at >= first) & (at < first + HALO), block, 0.0)
                grad_ref[ch, lay, :, cols] += block[HALO : HALO + tile]
                grad_ref[ch, lay, head, cols] += block[:HALO]
                grad_ref[ch, lay, tail, cols] += block[HALO + tile :]

    n_rows = gprobe.shape[0] // chunks
    half = n_rows // 2
    piece = half // group
    odd = lax.rem(my_c, 2)
    partner = (my_r, my_c + 1 - 2 * odd)
    place_in = my_r * n_half + my_c // 2

    def mate(k):
        other = lax.rem(place_in + k, group)
        return other, (other // n_half, 2 * lax.rem(other, n_half) + odd)

    def rows_at(start, size):
        return pl.ds(pl.multiple_of(start, piece), size)

    def wait_all(sem, ref):
        pltpu.make_async_copy(ref, ref, sem).wait()

    def owned(c, q):
        return rows_at(c * n_rows + odd * half + q * piece, piece)

    def pair_start(c):
        return send(
            gprobe.at[rows_at(c * n_rows + (1 - odd) * half, half)],
            half_in.at[c],
            pair_send,
            pair_recv,
            c,
            partner,
        )

    def scatter_start(c, copy):
        copy.wait()
        half_sum[c] = gprobe[rows_at(c * n_rows + odd * half, half)] + half_in[c]

        @pl.loop(1, group)
        def _(k):
            other, where = mate(k)
            send(
                half_sum.at[c, rows_at(other * piece, piece)],
                parts.at[c, rows_at((k - 1) * piece, piece)],
                rs_send,
                rs_recv,
                c,
                where,
            )

    def gather_start(c):
        wait_all(rs_recv.at[c], parts.at[c])
        value = half_sum[c, rows_at(place_in * piece, piece)]
        for k in range(group - 1):
            value = value + parts[c, pl.ds(k * piece, piece)]
        own = owned(c, place_in)
        total[own] = value

        @pl.loop(1, group)
        def _(k):
            pltpu.make_async_remote_copy(
                src_ref=total.at[own],
                dst_ref=total.at[own],
                send_sem=ag_send.at[c],
                recv_sem=ag_recv.at[c, k],
                device_id=mate(k)[1],
                device_id_type=MESH,
            ).start()

        send(total.at[own], total.at[own], fw_send, fw_recv, c, partner)

    def forward_start(c):
        @pl.loop(1, group)
        def _(k):
            got = total.at[owned(c, lax.rem(place_in + group - k, group))]
            wait_all(ag_recv.at[c, k], got)
            send(got, got, fw_send, fw_recv, c, partner)

    for p in range(2):

        @pl.loop(0, scans)
        def _(s):
            first_half(p, s)

    place(1)
    pl.semaphore_wait(barrier, n_dev - 1)
    copies_1 = grads_start(1)

    @pl.loop(0, scans)
    def _(s):
        second_half(0, s)

    early = chunks == 2
    pair_copy = pair_start(0) if early else None
    for s in range(scans):
        second_half(1, s)
        if early and s == 0:
            scatter_start(0, pair_copy)
        if early and s == scans - 1:
            gather_start(0)
    late = chunks - 1
    pair_copy = pair_start(late)
    place(0)
    copies_0 = grads_start(0)
    scatter_start(late, pair_copy)
    if early:
        forward_start(0)
    grads_end(1, copies_1)
    gather_start(late)
    grads_end(0, copies_0)
    forward_start(late)
    for c in range(chunks):
        wait_all(fw_recv.at[c], half_in.at[c])
    full = total[...]
    scale = STEP_SIZE / jnp.sqrt(jnp.sum(full * full, keepdims=True) / full.size + EPSILON)
    for p in range(2):
        for part in range(2):
            for m in range(2):
                at = rows_of(p, win)[part][m]
                new_ref[part, 2 * p + m] = (
                    probe_ref[part, 2 * p + m] - scale * total[pl.ds(at, win)]
                )
    for c in range(chunks):
        wait_all(rs_send.at[c], parts.at[c])
        wait_all(ag_send.at[c], parts.at[c])
        wait_all(fw_send.at[c], half_in.at[c])


def on_device(object_tiles, probe_modes, offsets, amplitude):
    n_row, n_col = lax.axis_size("row"), lax.axis_size("col")
    n_dev = n_row * n_col
    tile, win, scans = object_tiles.shape[2], probe_modes.shape[2], offsets.shape[2]
    tall, wide = tile + 2 * HALO, tile + LANES
    g_rows = 2 * probe_modes.shape[1] * win
    chunks = 2 if g_rows // 2 % (8 * n_dev) == 0 else 1
    half = g_rows // chunks // 2
    group = n_dev // 2
    vmem = pl.BlockSpec(memory_space=pltpu.VMEM)
    smem = pl.BlockSpec(memory_space=pltpu.SMEM)
    dma = pltpu.SemaphoreType.DMA
    side = pltpu.VMEM((tall, LANES), F32)
    sides = pltpu.VMEM((2, tall, LANES), F32)
    wide_tile = jax.ShapeDtypeStruct((2, 2, tall + SUB, wide), F32)
    limit = 40 * 1024 * 1024
    ext = pl.pallas_call(
        functools.partial(halo_kernel, (n_row, n_col)),
        out_shape=wide_tile,
        in_specs=[vmem],
        out_specs=vmem,
        scratch_shapes=[
            pltpu.VMEM((tile, LANES), F32),
            pltpu.VMEM((tile, LANES), F32),
            side,
            side,
            dma((8,)),
            dma((8,)),
        ],
        compiler_params=pltpu.CompilerParams(
            collective_id=0, has_side_effects=True, vmem_limit_bytes=limit
        ),
    )(object_tiles)
    winds = pl.pallas_call(
        functools.partial(window_kernel, (win, scans)),
        out_shape=jax.ShapeDtypeStruct((scans, 4, win, win), F32),
        in_specs=[smem, vmem],
        out_specs=vmem,
        compiler_params=pltpu.CompilerParams(vmem_limit_bytes=limit),
    )(offsets, ext)
    return pl.pallas_call(
        functools.partial(main_kernel, (n_row, n_col, win, scans, chunks)),
        out_shape=(
            jax.ShapeDtypeStruct(object_tiles.shape, F32),
            jax.ShapeDtypeStruct(probe_modes.shape, F32),
        ),
        in_specs=[smem] + [vmem] * 4,
        out_specs=(vmem, vmem),
        scratch_shapes=[
            pltpu.VMEM((scans, 2, 2 * win, 2 * win), F32),
            pltpu.VMEM((scans, 2, 2 * win, 2 * win), F32),
            pltpu.VMEM((scans, win, win), F32),
            pltpu.VMEM((2, 2, scans, win, win), F32),
            pltpu.VMEM((g_rows, win), F32),
            pltpu.VMEM((2, 2, tall, wide), F32),
            pltpu.VMEM((g_rows, win), F32),
            pltpu.VMEM((2, scans * win, 2 * wide), BF16),
            pltpu.VMEM((2, 2, HALO, tile), F32),
            pltpu.VMEM((2, 2, HALO, tile), F32),
            sides,
            sides,
            sides,
            sides,
            pltpu.VMEM((chunks, half, win), F32),
            pltpu.VMEM((chunks, half, win), F32),
            pltpu.VMEM((chunks, half - half // group, win), F32),
            dma((2, 8)),
            dma((2, 8)),
            dma((chunks,)),
            dma((chunks,)),
            dma((chunks,)),
            dma((chunks,)),
            dma((chunks,)),
            dma((chunks, group)),
            dma((chunks,)),
            dma((chunks,)),
        ],
        compiler_params=pltpu.CompilerParams(
            collective_id=1, has_side_effects=True, vmem_limit_bytes=limit
        ),
    )(offsets, winds, probe_modes, amplitude, jnp.asarray(tables(win)))


def solution(mesh):
    placed = (
        P(None, None, "row", "col"),
        P(),
        P("row", "col", None, None),
        P("row", "col", None, None, None),
    )
    return jax.shard_map(
        on_device,
        mesh=mesh,
        in_specs=placed,
        out_specs=(P(None, None, "row", "col"), P()),
        check_vma=False,
    )
```

```python
import functools

import jax
import jax.numpy as jnp
import numpy as np
from jax import lax
from jax.experimental import pallas as pl
from jax.experimental.pallas import tpu as pltpu
from jax.sharding import PartitionSpec as P

HALO = 32
PROP = 0.002
SHIFT_AMP = 0.5
STEP_SIZE = 0.5
EPSILON = 1e-06
LANES = 128
SUB = 8
MESH = pl.DeviceIdType.MESH
F32 = jnp.float32
BF16 = jnp.bfloat16


def tables(win):
    k = np.arange(win)
    c = np.exp(-2j * np.pi * (k[:, None] * k[None, :] % win) / win) / np.sqrt(win)
    freq = (k + win // 2) % win - win // 2
    kern = np.conj(c) @ np.diag(np.exp(-1j * PROP * freq**2)) @ c
    out = []
    for m in (c, np.conj(c), kern, np.conj(kern)):
        full = np.block([[m.real, m.imag], [-m.imag, m.real]])
        high = full.astype(np.float32).astype(jnp.bfloat16)
        low = (full - high.astype(np.float64)).astype(np.float32).astype(jnp.bfloat16)
        out += [high, low]
    return np.stack(out)


FWD, INV, KER, KER_INV = 0, 1, 2, 3


def split(x):
    high = x.astype(BF16)
    return high, (x - high.astype(F32)).astype(BF16)


def dot(a, b):
    return jnp.dot(a, b, preferred_element_type=F32)


def right(x, tab, which):
    high, low = split(x)
    return dot(high, tab[2 * which]) + (
        dot(low, tab[2 * which]) + dot(high, tab[2 * which + 1])
    )


def left(x, tab, which):
    high, low = split(x)
    which = which ^ 1
    return dot(tab[2 * which], high) + (
        dot(tab[2 * which], low) + dot(tab[2 * which + 1], high)
    )


def swap(y):
    w = y.shape[0] // 2
    top = jnp.concatenate([y[:w, :w], y[w:, :w]], axis=1)
    low = jnp.concatenate([y[:w, w:], y[w:, w:]], axis=1)
    return jnp.concatenate([top, low], axis=0)


def twice(x, axis):
    return jnp.concatenate([x, x], axis=axis)


def lane(rows):
    return lax.broadcasted_iota(jnp.int32, (rows, LANES), 1)


CHANS = [(part, lay) for part in range(2) for lay in range(2)]
EVERY = slice(None)


def packed(get, first, rows, count=4):
    out = None
    for ch in range(count):
        shift = (HALO * ch - first) % LANES
        block = get(ch)
        block = pltpu.roll(block, shift, 1) if shift else block
        at = lane(rows)
        keep = (at >= HALO * ch) & (at < HALO * ch + HALO)
        out = jnp.where(keep, block, 0.0 if out is None else out)
    return out


def unpacked(block, ch, first):
    shift = (first - HALO * ch) % LANES
    return pltpu.roll(block, shift, 1) if shift else block


def send(src, dst, ssem, rsem, i, to):
    copy = pltpu.make_async_remote_copy(
        src_ref=src,
        dst_ref=dst,
        send_sem=ssem.at[i],
        recv_sem=rsem.at[i],
        device_id=to,
        device_id_type=MESH,
    )
    copy.start()
    return copy


def places(n_row, n_col):
    my_r = lax.axis_index("row")
    my_c = lax.axis_index("col")
    up = lax.rem(my_r + n_row - 1, n_row)
    down = lax.rem(my_r + 1, n_row)
    lft = lax.rem(my_c + n_col - 1, n_col)
    rgt = lax.rem(my_c + 1, n_col)
    return my_r, my_c, up, down, lft, rgt


def zones(tile):
    head, tail = pl.ds(0, HALO), pl.ds(tile - HALO, HALO)
    mid, after, body = pl.ds(HALO, tile), pl.ds(HALO + tile, HALO), pl.ds(0, tile)
    return head, tail, mid, after, body


def rows_of(p, win):
    return [[(4 * p + 2 * part + m) * win for m in range(2)] for part in range(2)]


def halo_kernel(
    sizes, obj_ref, ext, pack_l, pack_r, halo_l, halo_r, h_send, h_recv
):
    n_row, n_col = sizes
    tile = obj_ref.shape[2]
    tall = tile + 2 * HALO
    wide = tile + LANES
    my_r, my_c, up, down, lft, rgt = places(n_row, n_col)
    head, tail, mid, after, body = zones(tile)
    barrier = pltpu.get_barrier_semaphore()
    around = [(r, c) for r in (up, my_r, down) for c in (lft, my_c, rgt)]
    del around[4]
    for to in around:
        pl.semaphore_signal(barrier, inc=1, device_id=to, device_id_type=MESH)
    pack_l[...] = packed(lambda ch: obj_ref[CHANS[ch] + (EVERY, slice(0, LANES))], 0, tile)
    pack_r[...] = packed(
        lambda ch: obj_ref[CHANS[ch] + (EVERY, slice(tile - LANES, tile))], LANES - HALO, tile
    )
    pl.semaphore_wait(barrier, 8)
    halo = [
        send(obj_ref.at[:, :, tail, :], ext.at[:, :, head, body], h_send, h_recv, 0, (down, my_c)),
        send(obj_ref.at[:, :, head, :], ext.at[:, :, after, body], h_send, h_recv, 1, (up, my_c)),
        send(pack_r, halo_l.at[mid], h_send, h_recv, 2, (my_r, rgt)),
        send(pack_l, halo_r.at[mid], h_send, h_recv, 3, (my_r, lft)),
        send(pack_r.at[tail], halo_l.at[head], h_send, h_recv, 4, (down, rgt)),
        send(pack_r.at[head], halo_l.at[after], h_send, h_recv, 5, (up, rgt)),
        send(pack_l.at[tail], halo_r.at[head], h_send, h_recv, 6, (down, lft)),
        send(pack_l.at[head], halo_r.at[after], h_send, h_recv, 7, (up, lft)),
    ]
    ext[:, :, mid, body] = obj_ref[...]
    ext[:, :, pl.ds(tall, SUB), :] = jnp.zeros((2, 2, SUB, wide), F32)
    for copy in halo:
        copy.wait()
    for ch in range(4):
        near = unpacked(halo_r[...], ch, 0)
        far_side = unpacked(halo_l[...], ch, LANES - HALO)
        at = lane(tall)
        edge = jnp.where(at < HALO, near, jnp.where(at >= LANES - HALO, far_side, 0.0))
        ext[CHANS[ch] + (pl.ds(0, tall), pl.ds(tile, LANES))] = edge


def window_kernel(sizes, off_ref, ext, winds):
    win, scans = sizes
    wide = ext.shape[3]

    @pl.loop(0, scans)
    def _(s):
        row = off_ref[0, 0, 0, s]
        base = pl.multiple_of(row - lax.rem(row, SUB), SUB)
        rest = lax.rem(win + SUB - lax.rem(row, SUB), win + SUB)
        shift = lax.rem(wide + HALO - off_ref[0, 0, 1, s], wide)
        for ch, (part, lay) in enumerate(CHANS):
            block = ext[part, lay, pl.ds(base, win + SUB), :]
            block = pltpu.roll(block, shift, 1)[:, :win]
            winds[s, ch] = pltpu.roll(block, rest, 0)[:win]


def main_kernel(
    sizes,
    off_ref,
    winds,
    probe_ref,
    amp_ref,
    tab,
    grad_ref,
    new_ref,
    wave,
    far,
    factor,
    gobj,
    gprobe,
    acc,
    total,
    spread,
    from_top,
    from_bot,
    edge_l,
    edge_r,
    from_l,
    from_r,
    half_in,
    half_sum,
    parts,
    g_send,
    g_recv,
    pair_send,
    pair_recv,
    rs_send,
    rs_recv,
    ag_send,
    ag_recv,
    fw_send,
    fw_recv,
):
    n_row, n_col, win, scans, chunks = sizes
    n_dev = n_row * n_col
    n_half = n_col // 2
    group = n_row * n_half
    tile = grad_ref.shape[2]
    tall, wide = tile + 2 * HALO, tile + LANES
    my_r, my_c, up, down, lft, rgt = places(n_row, n_col)
    head, tail, mid, after, body = zones(tile)
    me = my_r * n_col + my_c
    barrier = pltpu.get_barrier_semaphore()

    @pl.loop(1, n_dev)
    def _(k):
        other = lax.rem(me + k, n_dev)
        where = (other // n_col, lax.rem(other, n_col))
        pl.semaphore_signal(barrier, inc=1, device_id=where, device_id_type=MESH)

    gprobe[...] = jnp.zeros_like(gprobe)
    gobj[...] = jnp.zeros_like(gobj)

    @pl.loop(0, scans)
    def _(s):
        o = {chan: winds[s, ch] for ch, chan in enumerate(CHANS)}
        power = None
        for p in range(2):
            rows = []
            for m in range(2):
                pr, pi = probe_ref[0, 2 * p + m], probe_ref[1, 2 * p + m]
                rows.append(
                    jnp.concatenate(
                        [
                            pr * o[0, 0] - pi * o[1, 0],
                            pr * o[1, 0] + pi * o[0, 0],
                        ],
                        axis=1,
                    )
                )
            psi = jnp.concatenate(rows, axis=0)
            w = left(swap(right(psi, tab, KER)), tab, KER)
            wave[s, p] = w
            wr, wi = w[:win], w[win:]
            o1r, o1i = twice(o[0, 1], 1), twice(o[1, 1], 1)
            psi = jnp.concatenate([wr * o1r - wi * o1i, wr * o1i + wi * o1r], axis=0)
            psi = right(swap(left(psi, tab, FWD)), tab, FWD)
            far[s, p] = psi
            sq = psi * psi
            part_sum = (sq[:win, :win] + sq[:win, win:]) + (sq[win:, :win] + sq[win:, win:])
            power = part_sum if power is None else power + part_sum
        root = jnp.sqrt(power + SHIFT_AMP)
        factor[s] = 2.0 * (root - amp_ref[0, 0, s]) / root


    def first_half(p, s):
        g = far[s, p] * twice(twice(factor[s], 0), 1)
        g = left(swap(right(g, tab, INV)), tab, INV)
        w = wave[s, p]
        gr, gi, wr, wi = g[:win], g[win:], w[:win], w[win:]
        re = wr * gr + wi * gi
        im = wr * gi - wi * gr
        gobj[1, 0, s] += re[:, :win] + re[:, win:]
        gobj[1, 1, s] += im[:, :win] + im[:, win:]
        o1r, o1i = twice(winds[s, 1], 1), twice(winds[s, 3], 1)
        far[s, p] = jnp.concatenate([o1r * gr + o1i * gi, o1r * gi - o1i * gr], axis=0)

    def second_half(p, s):
        g = right(swap(left(far[s, p], tab, KER_INV)), tab, KER_INV)
        o0r, o0i = winds[s, 0], winds[s, 2]
        re = im = None
        for m in range(2):
            gr, gi = g[m * win : (m + 1) * win, :win], g[m * win : (m + 1) * win, win:]
            pr, pi = probe_ref[0, 2 * p + m], probe_ref[1, 2 * p + m]
            a = pr * gr + pi * gi
            b = pr * gi - pi * gr
            re, im = (a, b) if re is None else (re + a, im + b)
            at = rows_of(p, win)
            gprobe[pl.ds(at[0][m], win)] += o0r * gr + o0i * gi
            gprobe[pl.ds(at[1][m], win)] += o0r * gi - o0i * gr
        gobj[0, 0, s] += re
        gobj[0, 1, s] += im

    def one_hot(at, target):
        return jnp.where(at == target, 1.0, 0.0).astype(BF16)

    def place(lay):
        for s in range(scans):
            k = lax.broadcasted_iota(jnp.int32, (win, wide), 0) + (off_ref[0, 0, 1, s] - HALO)
            k = jnp.where(k < 0, k + wide, k)
            cols = one_hot(lax.broadcasted_iota(jnp.int32, (win, wide), 1), k)
            for part in range(2):
                for t, term in enumerate(split(gobj[lay, part, s])):
                    spread[t, pl.ds(s * win, win), pl.ds(part * wide, wide)] = dot(
                        term, cols
                    ).astype(BF16)
        rows = []
        for s in range(scans):
            j = lax.broadcasted_iota(jnp.int32, (tall, win), 1) + off_ref[0, 0, 0, s]
            rows.append(one_hot(lax.broadcasted_iota(jnp.int32, (tall, win), 0), j))
        rows = jnp.concatenate(rows, axis=1)
        for part in range(2):
            cut = pl.ds(part * wide, wide)
            acc[part, lay] = dot(rows, spread[0, :, cut]) + dot(rows, spread[1, :, cut])

    def grads_start(lay):
        edge_of = lambda ch: acc[ch, lay, :, pl.ds(tile, LANES)]
        er, el, fl, fr = edge_r.at[lay], edge_l.at[lay], from_l.at[lay], from_r.at[lay]
        er[...] = packed(edge_of, 0, tall, 2)
        el[...] = packed(edge_of, LANES - HALO, tall, 2)
        ss, rs = g_send.at[lay], g_recv.at[lay]
        return [
            send(acc.at[:, lay, head, body], from_bot.at[lay], ss, rs, 0, (up, my_c)),
            send(acc.at[:, lay, after, body], from_top.at[lay], ss, rs, 1, (down, my_c)),
            send(er.at[mid], fl.at[mid], ss, rs, 2, (my_r, rgt)),
            send(el.at[mid], fr.at[mid], ss, rs, 3, (my_r, lft)),
            send(er.at[head], fl.at[after], ss, rs, 4, (up, rgt)),
            send(er.at[after], fl.at[head], ss, rs, 5, (down, rgt)),
            send(el.at[head], fr.at[after], ss, rs, 6, (up, lft)),
            send(el.at[after], fr.at[head], ss, rs, 7, (down, lft)),
        ]

    def grads_end(lay, copies):
        grad_ref[:, lay] = acc[:, lay, mid, body]
        for copy in copies:
            copy.wait()
        grad_ref[:, lay, head, :] += from_top[lay]
        grad_ref[:, lay, tail, :] += from_bot[lay]
        for ref, first, cols in (
            (from_l, 0, pl.ds(0, LANES)),
            (from_r, LANES - HALO, pl.ds(tile - LANES, LANES)),
        ):
            for ch in range(2):
                at = lane(tall)
                block = unpacked(ref[lay], ch, first)
                block = jnp.where((at >= first) & (at < first + HALO), block, 0.0)
                grad_ref[ch, lay, :, cols] += block[HALO : HALO + tile]
                grad_ref[ch, lay, head, cols] += block[:HALO]
                grad_ref[ch, lay, tail, cols] += block[HALO + tile :]

    n_rows = gprobe.shape[0] // chunks
    half = n_rows // 2
    piece = half // group
    odd = lax.rem(my_c, 2)
    partner = (my_r, my_c + 1 - 2 * odd)
    place_in = my_r * n_half + my_c // 2

    def mate(k):
        other = lax.rem(place_in + k, group)
        return other, (other // n_half, 2 * lax.rem(other, n_half) + odd)

    def rows_at(start, size):
        return pl.ds(pl.multiple_of(start, piece), size)

    def wait_all(sem, ref):
        pltpu.make_async_copy(ref, ref, sem).wait()

    def owned(c, q):
        return rows_at(c * n_rows + odd * half + q * piece, piece)

    def pair_start(c):
        return send(
            gprobe.at[rows_at(c * n_rows + (1 - odd) * half, half)],
            half_in.at[c],
            pair_send,
            pair_recv,
            c,
            partner,
        )

    def scatter_start(c, copy):
        copy.wait()
        half_sum[c] = gprobe[rows_at(c * n_rows + odd * half, half)] + half_in[c]

        @pl.loop(1, group)
        def _(k):
            other, where = mate(k)
            send(
                half_sum.at[c, rows_at(other * piece, piece)],
                parts.at[c, rows_at((k - 1) * piece, piece)],
                rs_send,
                rs_recv,
                c,
                where,
            )

    def gather_start(c):
        wait_all(rs_recv.at[c], parts.at[c])
        value = half_sum[c, rows_at(place_in * piece, piece)]
        for k in range(group - 1):
            value = value + parts[c, pl.ds(k * piece, piece)]
        own = owned(c, place_in)
        total[own] = value

        @pl.loop(1, group)
        def _(k):
            pltpu.make_async_remote_copy(
                src_ref=total.at[own],
                dst_ref=total.at[own],
                send_sem=ag_send.at[c],
                recv_sem=ag_recv.at[c, k],
                device_id=mate(k)[1],
                device_id_type=MESH,
            ).start()

        send(total.at[own], total.at[own], fw_send, fw_recv, c, partner)

    def forward_start(c):
        @pl.loop(1, group)
        def _(k):
            got = total.at[owned(c, lax.rem(place_in + group - k, group))]
            wait_all(ag_recv.at[c, k], got)
            send(got, got, fw_send, fw_recv, c, partner)

    early = chunks == 2
    late = chunks - 1

    @pl.loop(0, scans)
    def _(s):
        first_half(0, s)
        second_half(0, s)

    pl.semaphore_wait(barrier, n_dev - 1)
    pair_0 = pair_start(0) if early else None

    @pl.loop(0, scans)
    def _(s):
        first_half(1, s)

    if early:
        scatter_start(0, pair_0)
    place(1)
    copies_1 = grads_start(1)

    @pl.loop(0, scans)
    def _(s):
        second_half(1, s)

    pair_1 = pair_start(late)
    place(0)
    scatter_start(late, pair_1)
    if early:
        gather_start(0)
    copies_0 = grads_start(0)
    grads_end(1, copies_1)
    gather_start(late)
    if early:
        forward_start(0)
    grads_end(0, copies_0)
    forward_start(late)
    for c in range(chunks):
        wait_all(fw_recv.at[c], half_in.at[c])
    full = total[...]
    scale = STEP_SIZE / jnp.sqrt(jnp.sum(full * full, keepdims=True) / full.size + EPSILON)
    for p in range(2):
        for part in range(2):
            for m in range(2):
                at = rows_of(p, win)[part][m]
                new_ref[part, 2 * p + m] = (
                    probe_ref[part, 2 * p + m] - scale * total[pl.ds(at, win)]
                )
    for c in range(chunks):
        wait_all(rs_send.at[c], parts.at[c])
        wait_all(ag_send.at[c], parts.at[c])
        wait_all(fw_send.at[c], half_in.at[c])


def on_device(object_tiles, probe_modes, offsets, amplitude):
    n_row, n_col = lax.axis_size("row"), lax.axis_size("col")
    n_dev = n_row * n_col
    tile, win, scans = object_tiles.shape[2], probe_modes.shape[2], offsets.shape[2]
    tall, wide = tile + 2 * HALO, tile + LANES
    g_rows = 2 * probe_modes.shape[1] * win
    chunks = 2 if g_rows // 2 % (8 * n_dev) == 0 else 1
    half = g_rows // chunks // 2
    group = n_dev // 2
    vmem = pl.BlockSpec(memory_space=pltpu.VMEM)
    smem = pl.BlockSpec(memory_space=pltpu.SMEM)
    dma = pltpu.SemaphoreType.DMA
    side = pltpu.VMEM((tall, LANES), F32)
    sides = pltpu.VMEM((2, tall, LANES), F32)
    wide_tile = jax.ShapeDtypeStruct((2, 2, tall + SUB, wide), F32)
    limit = 40 * 1024 * 1024
    pairs = offsets.transpose(0, 1, 3, 2)
    ext = pl.pallas_call(
        functools.partial(halo_kernel, (n_row, n_col)),
        out_shape=wide_tile,
        in_specs=[vmem],
        out_specs=vmem,
        scratch_shapes=[
            pltpu.VMEM((tile, LANES), F32),
            pltpu.VMEM((tile, LANES), F32),
            side,
            side,
            dma((8,)),
            dma((8,)),
        ],
        compiler_params=pltpu.CompilerParams(
            collective_id=0, has_side_effects=True, vmem_limit_bytes=limit
        ),
    )(object_tiles)
    winds = pl.pallas_call(
        functools.partial(window_kernel, (win, scans)),
        out_shape=jax.ShapeDtypeStruct((scans, 4, win, win), F32),
        in_specs=[smem, vmem],
        out_specs=vmem,
        compiler_params=pltpu.CompilerParams(vmem_limit_bytes=limit),
    )(pairs, ext)
    return pl.pallas_call(
        functools.partial(main_kernel, (n_row, n_col, win, scans, chunks)),
        out_shape=(
            jax.ShapeDtypeStruct(object_tiles.shape, F32),
            jax.ShapeDtypeStruct(probe_modes.shape, F32),
        ),
        in_specs=[smem] + [vmem] * 4,
        out_specs=(vmem, vmem),
        scratch_shapes=[
            pltpu.VMEM((scans, 2, 2 * win, 2 * win), F32),
            pltpu.VMEM((scans, 2, 2 * win, 2 * win), F32),
            pltpu.VMEM((scans, win, win), F32),
            pltpu.VMEM((2, 2, scans, win, win), F32),
            pltpu.VMEM((g_rows, win), F32),
            pltpu.VMEM((2, 2, tall, wide), F32),
            pltpu.VMEM((g_rows, win), F32),
            pltpu.VMEM((2, scans * win, 2 * wide), BF16),
            pltpu.VMEM((2, 2, HALO, tile), F32),
            pltpu.VMEM((2, 2, HALO, tile), F32),
            sides,
            sides,
            sides,
            sides,
            pltpu.VMEM((chunks, half, win), F32),
            pltpu.VMEM((chunks, half, win), F32),
            pltpu.VMEM((chunks, half - half // group, win), F32),
            dma((2, 8)),
            dma((2, 8)),
            dma((chunks,)),
            dma((chunks,)),
            dma((chunks,)),
            dma((chunks,)),
            dma((chunks,)),
            dma((chunks, group)),
            dma((chunks,)),
            dma((chunks,)),
        ],
        compiler_params=pltpu.CompilerParams(
            collective_id=1, has_side_effects=True, vmem_limit_bytes=limit
        ),
    )(pairs, winds, probe_modes, amplitude, jnp.asarray(tables(win)))


def solution(mesh):
    placed = (
        P(None, None, "row", "col"),
        P(),
        P("row", "col", None, None),
        P("row", "col", None, None, None),
    )
    return jax.shard_map(
        on_device,
        mesh=mesh,
        in_specs=placed,
        out_specs=(P(None, None, "row", "col"), P()),
        check_vma=False,
    )
```
